32 devices in a mesh: prompt: 2 (over y), tensor: 4 (over z), ctx: 4 (over x, core).
Axes of the slice: x: 2, y: 2, z: 4, core: 2. Of those that a mesh axis runs over, the one named last changes fastest.
Arguments:
- hidden_in: bfloat16 [2048, 8192], P(('prompt', 'ctx', 'tensor')), parts along dimension 0, may hold values from -6 to 6
- norm_gain: float32 [8192], replicated, may hold values from 0.1 to 1.9
- weight_in: bfloat16 [8192, 3, 4096], P('ctx', None, 'tensor'), may hold values from -0.0625 to 0.0625
- filter_taps: float32 [256, 128], P('tensor'), may hold values from -0.6 to 0.6
- filter_decay: float32 [256], P('tensor'), may hold values from 0.003 to 0.3
- skip_gain: float32 [4096], P('tensor'), may hold values from -1 to 1
- tail_cache: bfloat16 [254, 4096], P('prompt', 'tensor'), parts along dimension 0, may hold values from -6 to 6
- output_weight: bfloat16 [4096, 8192], P(None, 'tensor'), may hold values from -0.09375 to 0.09375
Outputs:
- mixer_output: bfloat16 [2048, 8192], P(('prompt', 'ctx'), 'tensor'), parts along dimension 0
The draws below stay inside these ranges and needn't reach their ends.
There are 2 independent parts, one for each index of `prompt`. The reference program is written for one: setup_inputs(seed, part) draws one part's arguments, and reference() takes and returns one part's arrays. A program takes and returns all parts, laid end to end along the dimension named above; an argument that names none is the same for every part. Nothing has to cross between parts.
All inputs are finite; a program needn't handle non-finite values.
Results may differ from the reference program's by a relative error of at most 0.0095.
Values may be sent and summed in bfloat16 or wider, within the bound.
A program may use at most 256 MiB of HBM per device.

```python
import math
import jax
import jax.numpy as jnp
from jax import lax

D = 8192
C = 4096
GROUP = 16
TAPS = 128
GROUPS = 256
TOKENS = 1024


def levels(rng, extent, pieces, low, high):
    factor_of = 1.0
    for dim, blocks in pieces:
        heights = jax.random.uniform(jax.random.fold_in(jax.random.fold_in(rng, 6), dim), (blocks,), jnp.float32, low / len(pieces), high / len(pieces))
        factor_of = factor_of * jnp.repeat(jnp.exp(heights), extent[dim] // blocks).reshape((-1,) + (1,) * (len(extent) - 1 - dim))
    return factor_of


def bell_draw(stream_key, shape, scale, most, cuts=(), held_as=jnp.bfloat16):
    array = jax.random.normal(stream_key, shape, jnp.float32) * scale
    if len(cuts) > 0:
        array = levels(stream_key, shape, cuts, -0.22, 0.18) * array
    return jnp.clip(array, min=-most, max=most).astype(held_as)


def setup_inputs(seed: int = 0, part: int = 0) -> dict:
    key_list = jax.random.split(jax.random.key(seed), 9)
    part_splits = jax.random.split(jax.random.fold_in(key_list[8], part), 9)
    hidden_in = bell_draw(part_splits[0], (TOKENS, D), 1.0, 6.0, ((0, 16),))
    norm_gain = jnp.clip(1.0 + 0.18 * jax.random.normal(key_list[1], (D,), jnp.float32), 0.1, 1.9)
    weight_in = bell_draw(key_list[2], (D, 3, C), D ** -0.5, 0.0625, ((0, 4), (2, 4)))
    filter_taps = bell_draw(key_list[3], (GROUPS, TAPS), 0.1, 0.6, ((0, 4),), jnp.float32)
    filter_decay = jnp.clip(jnp.exp(math.log(0.3) - 4.6051702 * jax.random.uniform(key_list[4], (GROUPS,), jnp.float32) ** levels(key_list[4], (GROUPS,), ((0, 4),), -0.2, 0.2)), 0.003, 0.3)
    skip_gain = jnp.clip(jax.random.uniform(key_list[5], (C,), jnp.float32, -1.0, 1.0) * levels(key_list[5], (C,), ((0, 4),), -0.4, 0.0), -1.0, 1.0)
    tail_cache = bell_draw(part_splits[6], (TAPS - 1, C), 1.0, 6.0, ((1, 4),))
    output_weight = bell_draw(key_list[7], (C, D), C ** -0.5, 0.09375, ((1, 4),))
    return dict(hidden_in=hidden_in, norm_gain=norm_gain, weight_in=weight_in, filter_taps=filter_taps, filter_decay=filter_decay, skip_gain=skip_gain, tail_cache=tail_cache, output_weight=output_weight)


def normalize_rows(hidden_in, norm_gain):
    values = hidden_in.astype(jnp.float32)
    scaled = lax.rsqrt(lax.optimization_barrier(jnp.mean(values * values, axis=-1, keepdims=True)) + 1e-06)
    return (values * scaled * norm_gain[None, :]).astype(jnp.bfloat16)

def reference(hidden_in, norm_gain, weight_in, filter_taps, filter_decay, skip_gain, tail_cache, output_weight):
    normed = normalize_rows(hidden_in, norm_gain)
    qkv = jnp.dot(normed, weight_in.reshape(D, 3 * C), preferred_element_type=jnp.float32).reshape(TOKENS, 3, C)
    query = qkv[:, 0]
    product = (qkv[:, 1] * qkv[:, 2]).astype(jnp.bfloat16)
    lags = jnp.arange(TAPS).astype(jnp.float32)
    taps_full = filter_taps * jnp.exp(-filter_decay[:, None] * lags[None, :])
    channel_taps = jnp.repeat(taps_full, GROUP, axis=0)
    extended = jnp.concatenate([tail_cache, product], axis=0).astype(jnp.float32)

    def add_tap(position, running):
        weights = lax.dynamic_index_in_dim(channel_taps, position, 1, keepdims=False)
        shifted = lax.dynamic_slice_in_dim(extended, (TAPS - 1 - position).astype(jnp.int32), TOKENS, 0)
        return running + weights[None, :] * shifted
    filtered = lax.fori_loop(0, TAPS, add_tap, jnp.zeros((TOKENS, C), jnp.float32))
    gated = (query * (filtered + skip_gain[None, :] * product.astype(jnp.float32))).astype(jnp.bfloat16)
    return jnp.dot(gated, output_weight, preferred_element_type=jnp.float32).astype(jnp.bfloat16)
```

```python
import jax
import jax.numpy as jnp
from jax import lax
from jax.experimental import pallas as pl
from jax.experimental.pallas import tpu as pltpu
from jax.sharding import PartitionSpec as P

GROUP = 16
LANES = 128


def passed_along(value, axis, steps):
    count = lax.axis_size(axis)
    leading, last = (max(0, -steps), min(count, count - steps))
    return lax.ppermute(value, axis, [(source, source + steps) for source in range(leading, last)])


def normalize_rows(hidden_in, norm_gain):
    values = hidden_in.astype(jnp.float32)
    scaled = lax.rsqrt(jnp.mean(values * values, axis=-1, keepdims=True) + 1e-06)
    return (values * scaled * norm_gain[None, :]).astype(jnp.bfloat16)


def toeplitz_kernel(rows_ref, bands_ref):
    for group in range(bands_ref.shape[0]):
        row = jnp.broadcast_to(rows_ref[group : group + 1, :], bands_ref.shape[1:])
        bands_ref[group] = pltpu.roll(row, 0, 1, stride=1, stride_axis=0).astype(jnp.bfloat16)


def banded_taps(filter_taps, filter_decay):
    groups, tap_count = filter_taps.shape
    lags = jnp.arange(tap_count).astype(jnp.float32)
    taps_full = filter_taps * jnp.exp(-filter_decay[:, None] * lags[None, :])
    rows = jnp.concatenate(
        [
            jnp.zeros((groups, 1), jnp.float32),
            taps_full[:, ::-1],
            jnp.zeros((groups, tap_count - 1), jnp.float32),
        ],
        axis=1,
    )
    block = 8
    return pl.pallas_call(
        toeplitz_kernel,
        grid=(groups // block,),
        in_specs=[pl.BlockSpec((block, 2 * tap_count), lambda i: (i, 0))],
        out_specs=pl.BlockSpec((block, tap_count, 2 * tap_count), lambda i: (i, 0, 0)),
        out_shape=jax.ShapeDtypeStruct((groups, tap_count, 2 * tap_count), jnp.bfloat16),
        cost_estimate=pl.CostEstimate(
            flops=groups * tap_count * tap_count * 16,
            bytes_accessed=groups * tap_count * tap_count * 4,
            transcendentals=0,
        ),
    )(rows)


def filter_kernel(query_ref, before_ref, product_ref, skip_ref, bands_ref, gated_ref):
    taps = bands_ref.shape[1]
    rows = product_ref.shape[0]
    blocks = rows // taps
    extended = jnp.concatenate([before_ref[...], product_ref[...]], axis=0)
    windows = jnp.concatenate(
        [extended[b * taps : (b + 2) * taps] for b in range(blocks)], axis=1
    )
    lane = lax.broadcasted_iota(jnp.int32, windows.shape, 1)
    owner = lax.rem(lane, LANES) // GROUP
    total = jnp.zeros((taps, blocks * LANES), jnp.float32)
    for group in range(LANES // GROUP):
        own = jnp.where(owner == group, windows, jnp.zeros_like(windows))
        total = total + jnp.dot(bands_ref[group], own, preferred_element_type=jnp.float32)
    for b in range(blocks):
        span = pl.ds(b * taps, taps)
        filtered = total[:, b * LANES : (b + 1) * LANES]
        product = product_ref[span, :].astype(jnp.float32)
        query = query_ref[span, :].astype(jnp.float32)
        gated_ref[span, :] = (query * (filtered + skip_ref[...] * product)).astype(jnp.bfloat16)


def filtered_and_gated(query, before, product, skip_gain, bands):
    rows, channels = product.shape
    taps = bands.shape[1]
    per = LANES // GROUP
    column = lambda i: (0, i)
    return pl.pallas_call(
        filter_kernel,
        grid=(channels // LANES,),
        in_specs=[
            pl.BlockSpec((rows, LANES), column),
            pl.BlockSpec((taps, LANES), column),
            pl.BlockSpec((rows, LANES), column),
            pl.BlockSpec((1, LANES), column),
            pl.BlockSpec((per, taps, 2 * taps), lambda i: (i, 0, 0)),
        ],
        out_specs=pl.BlockSpec((rows, LANES), column),
        out_shape=jax.ShapeDtypeStruct((rows, channels), jnp.bfloat16),
    )(query, before, product, skip_gain.reshape(1, channels), bands)


def on_device(
    hidden_in, norm_gain, weight_in, filter_taps, filter_decay, skip_gain, tail_cache, output_weight
):
    rows, width = hidden_in.shape
    depth, _, channels = weight_in.shape
    taps = filter_taps.shape[1]
    normed = normalize_rows(hidden_in, norm_gain)
    parts = width // depth
    pieces = jnp.stack([normed[:, p * depth : (p + 1) * depth] for p in range(parts)])
    pieces = lax.all_to_all(pieces, "ctx", 0, 0, tiled=True)
    pieces = lax.all_gather(pieces, "tensor", axis=0)
    pieces = pieces.transpose(1, 0, 2, 3)
    shards = pieces.shape[1]
    pieces = pieces.reshape(parts * shards * rows, depth)
    planes = weight_in.transpose(1, 0, 2)

    def projected(which):
        partial = jnp.dot(pieces, planes[which], preferred_element_type=jnp.float32)
        return lax.psum_scatter(
            partial.astype(jnp.bfloat16), "ctx", scatter_dimension=0, tiled=True
        )

    key, value, query = (projected(which) for which in (1, 2, 0))
    product = (key.astype(jnp.float32) * value.astype(jnp.float32)).astype(jnp.bfloat16)
    incoming = passed_along(product[product.shape[0] - taps :], "ctx", 1)
    leading = lax.axis_index("ctx") == 0
    tail = jnp.concatenate([jnp.zeros((1, channels), jnp.bfloat16), tail_cache], axis=0)
    before = jnp.where(leading, tail, incoming)
    bands = banded_taps(filter_taps, filter_decay)
    gated = filtered_and_gated(query, before, product, skip_gain, bands)
    totals = jnp.dot(
        lax.all_gather(gated, "tensor", axis=1, tiled=True),
        output_weight,
        preferred_element_type=jnp.float32,
    )
    return totals.astype(jnp.bfloat16)


def solution(mesh):
    in_specs = (
        P(("prompt", "ctx", "tensor"), None),
        P(),
        P("ctx", None, "tensor"),
        P("tensor", None),
        P("tensor"),
        P("tensor"),
        P("prompt", "tensor"),
        P(None, "tensor"),
    )
    out_specs = P(("prompt", "ctx"), "tensor")
    return jax.shard_map(
        on_device, mesh=mesh, in_specs=in_specs, out_specs=out_specs, check_vma=False
    )
```

```python
import functools
import jax
import jax.numpy as jnp
from jax import lax
from jax.experimental import pallas as pl
from jax.experimental.pallas import tpu as pltpu
from jax.sharding import PartitionSpec as P

GROUP = 16
LANES = 128


def passed_along(value, axis, steps):
    count = lax.axis_size(axis)
    leading, last = (max(0, -steps), min(count, count - steps))
    return lax.ppermute(value, axis, [(source, source + steps) for source in range(leading, last)])


def normalize_rows(hidden_in, norm_gain):
    values = hidden_in.astype(jnp.float32)
    scaled = lax.rsqrt(jnp.mean(values * values, axis=-1, keepdims=True) + 1e-06)
    return (values * scaled * norm_gain[None, :]).astype(jnp.bfloat16)


def toeplitz_kernel(rows_ref, bands_ref):
    for group in range(bands_ref.shape[0]):
        row = jnp.broadcast_to(rows_ref[group : group + 1, :], bands_ref.shape[1:])
        bands_ref[group] = pltpu.roll(row, 0, 1, stride=1, stride_axis=0).astype(jnp.bfloat16)


def banded_taps(filter_taps, filter_decay):
    groups, tap_count = filter_taps.shape
    lags = jnp.arange(tap_count).astype(jnp.float32)
    taps_full = filter_taps * jnp.exp(-filter_decay[:, None] * lags[None, :])
    rows = jnp.concatenate(
        [
            jnp.zeros((groups, 1), jnp.float32),
            taps_full[:, ::-1],
            jnp.zeros((groups, tap_count - 1), jnp.float32),
        ],
        axis=1,
    )
    block = 8
    return pl.pallas_call(
        toeplitz_kernel,
        grid=(groups // block,),
        in_specs=[pl.BlockSpec((block, 2 * tap_count), lambda i: (i, 0))],
        out_specs=pl.BlockSpec((block, tap_count, 2 * tap_count), lambda i: (i, 0, 0)),
        out_shape=jax.ShapeDtypeStruct((groups, tap_count, 2 * tap_count), jnp.bfloat16),
        cost_estimate=pl.CostEstimate(
            flops=groups * tap_count * tap_count * 16,
            bytes_accessed=groups * tap_count * tap_count * 4,
            transcendentals=0,
        ),
    )(rows)


def filter_kernel(query_ref, before_ref, product_ref, skip_ref, bands_ref, gated_ref):
    taps = bands_ref.shape[1]
    rows = product_ref.shape[0]
    blocks = rows // taps
    extended = jnp.concatenate([before_ref[...], product_ref[...]], axis=0)
    windows = jnp.concatenate(
        [extended[b * taps : (b + 2) * taps] for b in range(blocks)], axis=1
    )
    lane = lax.broadcasted_iota(jnp.int32, windows.shape, 1)
    owner = lax.rem(lane, LANES) // GROUP
    total = jnp.zeros((taps, blocks * LANES), jnp.float32)
    for group in range(LANES // GROUP):
        own = jnp.where(owner == group, windows, jnp.zeros_like(windows))
        total = total + jnp.dot(bands_ref[group], own, preferred_element_type=jnp.float32)
    for b in range(blocks):
        span = pl.ds(b * taps, taps)
        filtered = total[:, b * LANES : (b + 1) * LANES]
        product = product_ref[span, :].astype(jnp.float32)
        query = query_ref[span, :].astype(jnp.float32)
        gated_ref[span, :] = (query * (filtered + skip_ref[...] * product)).astype(jnp.bfloat16)


def filtered_and_gated(query, before, product, skip_gain, bands):
    rows, channels = product.shape
    taps = bands.shape[1]
    per = LANES // GROUP
    column = lambda i: (0, i)
    return pl.pallas_call(
        filter_kernel,
        grid=(channels // LANES,),
        in_specs=[
            pl.BlockSpec((rows, LANES), column),
            pl.BlockSpec((taps, LANES), column),
            pl.BlockSpec((rows, LANES), column),
            pl.BlockSpec((1, LANES), column),
            pl.BlockSpec((per, taps, 2 * taps), lambda i: (i, 0, 0)),
        ],
        out_specs=pl.BlockSpec((rows, LANES), column),
        out_shape=jax.ShapeDtypeStruct((rows, channels), jnp.bfloat16),
    )(query, before, product, skip_gain.reshape(1, channels), bands)


MESH = pl.DeviceIdType.MESH


def greet(axis_peers):
    barrier = pltpu.get_barrier_semaphore()
    for axis, peer, there in axis_peers:

        @pl.when(there)
        def _(axis=axis, peer=peer):
            pl.semaphore_signal(barrier, inc=1, device_id={axis: peer}, device_id_type=MESH)

    pl.semaphore_wait(barrier, sum(jnp.where(there, 1, 0) for _, _, there in axis_peers))


def line_neighbours(count):
    place = lax.axis_index("tensor")
    return [
        ("tensor", jnp.maximum(place - 1, 0), place > 0),
        ("tensor", jnp.minimum(place + 1, count - 1), place < count - 1),
    ]


def hop(slots, origin, way, send_sem, recv_sem, count):
    place = lax.axis_index("tensor")
    target = jnp.clip(place + 2 * way - 1, 0, count - 1)
    return pltpu.make_async_remote_copy(
        src_ref=slots.at[origin],
        dst_ref=slots.at[origin],
        send_sem=send_sem.at[way, origin],
        recv_sem=recv_sem.at[origin],
        device_id={"tensor": target},
        device_id_type=MESH,
    )


def relay(slots, send_sem, recv_sem, count, use):
    place = lax.axis_index("tensor")

    def send(origin, way):
        @pl.when((place + 1 < count) if way else (place > 0))
        def _():
            hop(slots, origin, way, send_sem, recv_sem, count).start()

    send(place, 0)
    send(place, 1)
    use(place)

    def step(distance, carry):
        below, above = place - distance, place + distance

        @pl.when(below >= 0)
        def _():
            origin = jnp.maximum(below, 0)
            hop(slots, origin, 1, send_sem, recv_sem, count).wait_recv()
            send(origin, 1)

        @pl.when(above < count)
        def _():
            origin = jnp.minimum(above, count - 1)
            hop(slots, origin, 0, send_sem, recv_sem, count).wait_recv()
            send(origin, 0)

        @pl.when(below >= 0)
        def _():
            use(jnp.maximum(below, 0))

        @pl.when(above < count)
        def _():
            use(jnp.minimum(above, count - 1))

        return carry

    lax.fori_loop(1, count, step, 0)


def relay_sent(slots, send_sem, recv_sem, count):
    place = lax.axis_index("tensor")

    def step(origin, carry):
        @pl.when((origin <= place) & (place + 1 < count))
        def _():
            hop(slots, origin, 1, send_sem, recv_sem, count).wait_send()

        @pl.when((origin >= place) & (place > 0))
        def _():
            hop(slots, origin, 0, send_sem, recv_sem, count).wait_send()

        return carry

    lax.fori_loop(0, count, step, 0)


def project_kernel(
    shards,
    parts,
    normed_ref,
    planes_ref,
    query_ref,
    product_ref,
    planes,
    slots,
    partial,
    arrived,
    load_sem,
    own_sem,
    swap_send,
    swap_recv,
    line_send,
    line_recv,
    sum_send,
    sum_recv,
):
    rows = normed_ref.shape[0]
    _, depth, channels = planes.shape
    tile = min(256, channels)
    me, place = lax.axis_index("ctx"), lax.axis_index("tensor")
    others = [lax.rem(me + 1 + k, parts) for k in range(parts - 1)]
    loads = [
        pltpu.make_async_copy(planes_ref.at[g], planes.at[g], load_sem.at[g]) for g in (1, 2, 0)
    ]
    for load in loads:
        load.start()
    greet([("ctx", other, me >= 0) for other in others] + line_neighbours(shards))

    def span(index, size):
        return pl.ds(pl.multiple_of(index * size, size), size)

    swaps = [
        pltpu.make_async_remote_copy(
            src_ref=normed_ref.at[:, span(other, depth)],
            dst_ref=slots.at[place, span(me, rows)],
            send_sem=swap_send.at[k],
            recv_sem=swap_recv.at[parts - 2 - k],
            device_id={"ctx": other},
            device_id_type=MESH,
        )
        for k, other in enumerate(others)
    ]
    for swap in swaps:
        swap.start()
    own = pltpu.make_async_copy(
        normed_ref.at[:, span(me, depth)], slots.at[place, span(me, rows)], own_sem
    )
    own.start()
    own.wait()
    for swap in swaps:
        swap.wait_recv()
    for load in loads:
        load.wait()

    def use(origin):
        def plane(step, carry):
            g = lax.rem(step + 1, 3)

            def columns(index, inner):
                where = span(index, tile)
                partial[g, origin, :, where] = jnp.dot(
                    slots[origin], planes[g, :, where], preferred_element_type=jnp.float32
                ).astype(jnp.bfloat16)
                return inner

            lax.fori_loop(0, channels // tile, columns, 0)
            for k, other in enumerate(others):
                pltpu.make_async_remote_copy(
                    src_ref=partial.at[g, origin, span(other, rows)],
                    dst_ref=arrived.at[g, parts - 2 - k, span(origin, rows)],
                    send_sem=sum_send,
                    recv_sem=sum_recv.at[g],
                    device_id={"ctx": other},
                    device_id_type=MESH,
                ).start()
            return carry

        lax.fori_loop(0, 3, plane, 0)

    relay(slots, line_send, line_recv, shards, use)

    def total(g, origin):
        value = partial[g, origin, span(me, rows)].astype(jnp.float32)
        for k in range(parts - 1):
            value = value + arrived[g, k, span(origin, rows)].astype(jnp.float32)
        return value

    for g in (1, 2):
        pltpu.make_async_copy(arrived.at[g], arrived.at[g], sum_recv.at[g]).wait()

    def write_product(origin, carry):
        product_ref[span(origin, rows), :] = (total(1, origin) * total(2, origin)).astype(
            jnp.bfloat16
        )
        return carry

    lax.fori_loop(0, shards, write_product, 0)
    pltpu.make_async_copy(arrived.at[0], arrived.at[0], sum_recv.at[0]).wait()

    def write_query(origin, carry):
        query_ref[span(origin, rows), :] = total(0, origin)
        return carry

    lax.fori_loop(0, shards, write_query, 0)
    for swap in swaps:
        swap.wait_send()
    relay_sent(slots, line_send, line_recv, shards)
    pltpu.make_async_copy(arrived, arrived, sum_send).wait()


def projected(normed, planes):
    shards, parts = lax.axis_size("tensor"), lax.axis_size("ctx")
    rows = normed.shape[0]
    _, depth, channels = planes.shape
    vmem = pl.BlockSpec(memory_space=pltpu.VMEM)
    dma = pltpu.SemaphoreType.DMA
    return pl.pallas_call(
        functools.partial(project_kernel, shards, parts),
        out_shape=(
            jax.ShapeDtypeStruct((shards * rows, channels), jnp.float32),
            jax.ShapeDtypeStruct((shards * rows, channels), jnp.bfloat16),
        ),
        in_specs=[vmem, pl.BlockSpec(memory_space=pl.ANY)],
        out_specs=(vmem, vmem),
        scratch_shapes=[
            pltpu.VMEM((3, depth, channels), jnp.bfloat16),
            pltpu.VMEM((shards, parts * rows, depth), jnp.bfloat16),
            pltpu.VMEM((3, shards, parts * rows, channels), jnp.bfloat16),
            pltpu.VMEM((3, parts - 1, shards * rows, channels), jnp.bfloat16),
            dma((3,)),
            dma,
            dma((parts - 1,)),
            dma((parts - 1,)),
            dma((2, shards)),
            dma((shards,)),
            dma,
            dma((3,)),
        ],
        compiler_params=pltpu.CompilerParams(
            collective_id=0, has_side_effects=True, vmem_limit_bytes=44 << 20
        ),
    )(normed, planes)


def output_kernel(
    shards, gated_ref, weight_ref, out_ref, weight, slots, total, load_sem, own_sem, line_send, line_recv
):
    channels = gated_ref.shape[1]
    columns = out_ref.shape[1]
    tile = min(256, columns)
    place = lax.axis_index("tensor")
    load = pltpu.make_async_copy(weight_ref, weight, load_sem)
    load.start()
    own = pltpu.make_async_copy(gated_ref, slots.at[place], own_sem)
    own.start()
    greet(line_neighbours(shards))
    own.wait()
    total[...] = jnp.zeros_like(total)

    def use(origin):
        deep = pl.ds(pl.multiple_of(origin * channels, channels), channels)

        def column(index, carry):
            where = pl.ds(pl.multiple_of(index * tile, tile), tile)
            total[:, where] += jnp.dot(
                slots[origin], weight[deep, where], preferred_element_type=jnp.float32
            )
            return carry

        lax.fori_loop(0, columns // tile, column, 0)

    load.wait()
    relay(slots, line_send, line_recv, shards, use)
    out_ref[...] = total[...].astype(jnp.bfloat16)
    relay_sent(slots, line_send, line_recv, shards)


def output_projection(gated, output_weight):
    shards = lax.axis_size("tensor")
    rows, channels = gated.shape
    depth, columns = output_weight.shape
    vmem = pl.BlockSpec(memory_space=pltpu.VMEM)
    dma = pltpu.SemaphoreType.DMA
    return pl.pallas_call(
        functools.partial(output_kernel, shards),
        out_shape=jax.ShapeDtypeStruct((rows, columns), jnp.bfloat16),
        in_specs=[vmem, pl.BlockSpec(memory_space=pl.ANY)],
        out_specs=vmem,
        scratch_shapes=[
            pltpu.VMEM((depth, columns), jnp.bfloat16),
            pltpu.VMEM((shards, rows, channels), jnp.bfloat16),
            pltpu.VMEM((rows, columns), jnp.float32),
            dma,
            dma,
            dma((2, shards)),
            dma((shards,)),
        ],
        compiler_params=pltpu.CompilerParams(
            collective_id=1, has_side_effects=True, vmem_limit_bytes=44 << 20
        ),
    )(gated, output_weight)


def on_device(
    hidden_in, norm_gain, weight_in, filter_taps, filter_decay, skip_gain, tail_cache, output_weight
):
    channels = weight_in.shape[2]
    taps = filter_taps.shape[1]
    bands = banded_taps(filter_taps, filter_decay)
    normed = normalize_rows(hidden_in, norm_gain)
    query, product = projected(normed, weight_in.transpose(1, 0, 2))
    incoming = passed_along(product[product.shape[0] - taps :], "ctx", 1)
    leading = lax.axis_index("ctx") == 0
    tail = jnp.concatenate([jnp.zeros((1, channels), jnp.bfloat16), tail_cache], axis=0)
    before = jnp.where(leading, tail, incoming)
    gated = filtered_and_gated(query, before, product, skip_gain, bands)
    return output_projection(gated, output_weight)


def solution(mesh):
    in_specs = (
        P(("prompt", "ctx", "tensor"), None),
        P(),
        P("ctx", None, "tensor"),
        P("tensor", None),
        P("tensor"),
        P("tensor"),
        P("prompt", "tensor"),
        P(None, "tensor"),
    )
    out_specs = P(("prompt", "ctx"), "tensor")
    return jax.shard_map(
        on_device, mesh=mesh, in_specs=in_specs, out_specs=out_specs, check_vma=False
    )
```

```python
import functools

import jax
import jax.numpy as jnp
from jax import lax
from jax.experimental import pallas as pl
from jax.experimental.pallas import tpu as pltpu
from jax.sharding import PartitionSpec as P

GROUP = 16
LANES = 128
MESH = pl.DeviceIdType.MESH


def normalize_rows(hidden_in, norm_gain):
    values = hidden_in.astype(jnp.float32)
    scaled = lax.rsqrt(jnp.mean(values * values, axis=-1, keepdims=True) + 1e-06)
    return (values * scaled * norm_gain[None, :]).astype(jnp.bfloat16)


def first_rows(filter_taps, filter_decay):
    groups, tap_count = filter_taps.shape
    lags = jnp.arange(tap_count).astype(jnp.float32)
    taps_full = filter_taps * jnp.exp(-filter_decay[:, None] * lags[None, :])
    return jnp.pad(taps_full[:, ::-1], ((0, 0), (1, tap_count - 1)))


def span(index, size):
    return pl.ds(pl.multiple_of(index * size, size), size)


def greet(peers):
    barrier = pltpu.get_barrier_semaphore()
    for axis, peer, there in peers:

        @pl.when(there)
        def _(axis=axis, peer=peer):
            pl.semaphore_signal(barrier, inc=1, device_id={axis: peer}, device_id_type=MESH)

    pl.semaphore_wait(barrier, sum(jnp.where(there, 1, 0) for _, _, there in peers))


class Line:
    def __init__(self, count, pieces, view, send_sem, recv_sem):
        self.count, self.pieces, self.view = count, pieces, view
        self.send_sem, self.recv_sem = send_sem, recv_sem
        self.place = lax.axis_index("tensor")

    def inside(self, position):
        return (position >= 0) & (position < self.count)

    def hop(self, origin, piece, up):
        ref = self.view(origin, piece)
        return pltpu.make_async_remote_copy(
            src_ref=ref,
            dst_ref=ref,
            send_sem=self.send_sem.at[up, origin, piece],
            recv_sem=self.recv_sem.at[origin, piece],
            device_id={"tensor": jnp.clip(self.place + 2 * up - 1, 0, self.count - 1)},
            device_id_type=MESH,
        )

    def send(self, origin, piece, up):
        @pl.when(self.inside(self.place + 2 * up - 1))
        def _():
            self.hop(origin, piece, up).start()

    def pass_on(self, distance, piece, up):
        origin = self.place - distance * (2 * up - 1)

        @pl.when(self.inside(origin))
        def _():
            source = jnp.clip(origin, 0, self.count - 1)
            self.hop(source, piece, up).wait_recv()
            self.send(source, piece, up)

    def sent(self):
        def step(index, carry):
            origin, piece = index // self.pieces, lax.rem(index, self.pieces)

            @pl.when((origin <= self.place) & (self.place + 1 < self.count))
            def _():
                self.hop(origin, piece, 1).wait_send()

            @pl.when((origin >= self.place) & (self.place > 0))
            def _():
                self.hop(origin, piece, 0).wait_send()

            return carry

        lax.fori_loop(0, self.count * self.pieces, step, 0)


def mixer_kernel(
    shards,
    parts,
    normed_ref,
    planes_ref,
    first_ref,
    skip_ref,
    tail_ref,
    weight_ref,
    out_ref,
    planes,
    slots,
    partial,
    arrived,
    query,
    product,
    before,
    bands,
    weight,
    gated,
    total,
    load_sem,
    own_sem,
    swap_send,
    swap_recv,
    line_send,
    line_recv,
    sum_send,
    sum_recv,
    tail_send,
    tail_recv,
    gated_send,
    gated_recv,
):
    rows = normed_ref.shape[0]
    _, depth, channels = planes.shape
    groups, taps, _ = bands.shape
    chunks, all_rows, chunk = gated.shape[1:]
    columns = out_ref.shape[1]
    tile = min(256, channels)
    me, place = lax.axis_index("ctx"), lax.axis_index("tensor")
    others = [lax.rem(me + 1 + k, parts) for k in range(parts - 1)]

    loads = [
        pltpu.make_async_copy(planes_ref.at[g], planes.at[g], load_sem.at[g]) for g in (1, 2, 0)
    ]
    for load in loads:
        load.start()
    own = pltpu.make_async_copy(
        normed_ref.at[:, span(me, depth)], slots.at[place, span(me, rows)], own_sem
    )
    own.start()
    last_load = pltpu.make_async_copy(weight_ref, weight, load_sem.at[3])
    last_load.start()
    tail_load = pltpu.make_async_copy(tail_ref, before, load_sem.at[4])

    @pl.when(me == 0)
    def _():
        tail_load.start()

    neighbours = [
        ("tensor", jnp.maximum(place - 1, 0), place > 0),
        ("tensor", jnp.minimum(place + 1, shards - 1), place < shards - 1),
    ]
    greet([("ctx", other, me >= 0) for other in others] + neighbours)

    swaps = [
        pltpu.make_async_remote_copy(
            src_ref=normed_ref.at[:, span(other, depth)],
            dst_ref=slots.at[place, span(me, rows)],
            send_sem=swap_send.at[k],
            recv_sem=swap_recv.at[parts - 2 - k],
            device_id={"ctx": other},
            device_id_type=MESH,
        )
        for k, other in enumerate(others)
    ]
    for swap in swaps:
        swap.start()
    line = Line(
        shards, parts, lambda origin, c: slots.at[origin, span(c, rows)], line_send, line_recv
    )
    own.wait()
    line.send(place, me, 0)
    line.send(place, me, 1)

    for k in range(parts - 1):
        swaps[parts - 2 - k].wait_recv()
        line.send(place, others[k], 0)
        line.send(place, others[k], 1)

    def write_band(group, carry):
        row = jnp.broadcast_to(first_ref[pl.ds(group, 1), :], (taps, 2 * taps))
        bands[group] = pltpu.roll(row, 0, 1, stride=1, stride_axis=0).astype(jnp.bfloat16)
        return carry

    lax.fori_loop(0, groups, write_band, 0)
    for load in loads:
        load.wait()

    tiles = channels // tile

    def project(origin, k):
        def step(index, carry):
            g, column = lax.rem(index // tiles + 1, 3), lax.rem(index, tiles)
            where = span(column, tile)
            partial[g, origin, :, where] = jnp.dot(
                slots[origin], planes[g, :, where], preferred_element_type=jnp.float32
            ).astype(jnp.bfloat16)

            @pl.when(column == tiles - 1)
            def _():
                for k, other in enumerate(others):
                    pltpu.make_async_remote_copy(
                        src_ref=partial.at[g, origin, span(other, rows)],
                        dst_ref=arrived.at[g, parts - 2 - k, span(origin, rows)],
                        send_sem=sum_send,
                        recv_sem=sum_recv.at[g],
                        device_id={"ctx": other},
                        device_id_type=MESH,
                    ).start()

            return carry

        steps = 3 * tiles
        lax.fori_loop(k * steps // parts, (k + 1) * steps // parts, step, 0)

    def project_from(distance, k):
        below, above = place - distance, place + distance

        @pl.when(line.inside(below))
        def _():
            project(jnp.maximum(below, 0), k)

        @pl.when(line.inside(above) & (distance > 0))
        def _():
            project(jnp.minimum(above, shards - 1), k)

    def stage(index, carry):
        distance, k = index // parts, lax.rem(index, parts)
        project_from(distance, k)

        @pl.when(distance + 1 < shards)
        def _():
            piece = lax.rem(me + k, parts)
            line.pass_on(distance + 1, piece, 1)
            line.pass_on(distance + 1, piece, 0)

        return carry

    lax.fori_loop(0, shards * parts, stage, 0)

    def summed(g, origin):
        value = partial[g, origin, span(me, rows)].astype(jnp.float32)
        for k in range(parts - 1):
            value = value + arrived[g, k, span(origin, rows)].astype(jnp.float32)
        return value

    for g in (1, 2):
        pltpu.make_async_copy(arrived.at[g], arrived.at[g], sum_recv.at[g]).wait()

    def write_product(step, carry):
        origin = shards - 1 - step
        product[span(origin, rows), :] = (summed(1, origin) * summed(2, origin)).astype(
            jnp.bfloat16
        )
        return carry

    tail_steps = -(-taps // rows)
    lax.fori_loop(0, tail_steps, write_product, 0)
    tail = pltpu.make_async_remote_copy(
        src_ref=product.at[pl.ds(all_rows - taps, taps)],
        dst_ref=before,
        send_sem=tail_send,
        recv_sem=tail_recv,
        device_id={"ctx": jnp.minimum(me + 1, parts - 1)},
        device_id_type=MESH,
    )

    @pl.when(me + 1 < parts)
    def _():
        tail.start()

    lax.fori_loop(tail_steps, shards, write_product, 0)
    pltpu.make_async_copy(arrived.at[0], arrived.at[0], sum_recv.at[0]).wait()

    def write_query(origin, carry):
        query[span(origin, rows), :] = summed(0, origin)
        return carry

    lax.fori_loop(0, shards, write_query, 0)

    @pl.when(me > 0)
    def _():
        tail.wait_recv()

    @pl.when(me == 0)
    def _():
        tail_load.wait()

    per, windows_count = LANES // GROUP, all_rows // taps

    def filter_lanes(block, c, offset):
        where = span(block, LANES)
        extended = jnp.concatenate([before[:, where], product[:, where]], axis=0)
        windows = jnp.concatenate(
            [extended[b * taps : (b + 2) * taps] for b in range(windows_count)], axis=1
        )
        lane = lax.broadcasted_iota(jnp.int32, windows.shape, 1)
        owner = lax.rem(lane, LANES) // GROUP
        filtered = jnp.zeros((taps, windows_count * LANES), jnp.float32)
        for group in range(per):
            mine = jnp.where(owner == group, windows, jnp.zeros_like(windows))
            filtered = filtered + jnp.dot(
                bands[block * per + group], mine, preferred_element_type=jnp.float32
            )
        for b in range(windows_count):
            inner = pl.ds(b * taps, taps)
            direct = skip_ref[:, where] * product[inner, where].astype(jnp.float32)
            gated[place, c, inner, pl.ds(offset, LANES)] = (
                query[inner, where] * (filtered[:, b * LANES : (b + 1) * LANES] + direct)
            ).astype(jnp.bfloat16)

    gated_line = Line(
        shards, chunks, lambda origin, c: gated.at[origin, c], gated_send, gated_recv
    )

    def filter_chunk(c, carry):
        for part in range(chunk // LANES):
            filter_lanes(c * (chunk // LANES) + part, c, part * LANES)
        gated_line.send(place, c, 0)
        gated_line.send(place, c, 1)
        return carry

    lax.fori_loop(0, chunks, filter_chunk, 0)
    last_load.wait()
    wide = min(512, columns)

    def multiply(origin, c, fresh):
        deep = span(origin * chunks + c, chunk)

        def column(index, carry):
            where = span(index, wide)
            value = jnp.dot(
                gated[origin, c], weight[deep, where], preferred_element_type=jnp.float32
            )
            total[:, where] = value if fresh else total[:, where] + value
            return carry

        lax.fori_loop(0, columns // wide, column, 0)

    multiply(place, 0, True)

    def multiply_own(c, carry):
        multiply(place, c, False)
        return carry

    lax.fori_loop(1, chunks, multiply_own, 0)
    first_up = jnp.where(2 * place >= shards, 1, 0)

    def collect(index, carry):
        distance, side = index // (2 * chunks) + 1, lax.rem(index // chunks, 2)
        c = lax.rem(index, chunks)
        up = lax.rem(first_up + side, 2)
        gated_line.pass_on(distance, c, up)
        origin = place - distance * (2 * up - 1)

        @pl.when(gated_line.inside(origin))
        def _():
            multiply(jnp.clip(origin, 0, shards - 1), c, False)

        return carry

    lax.fori_loop(0, 2 * chunks * (shards - 1), collect, 0)
    out_ref[...] = total[...].astype(jnp.bfloat16)

    for swap in swaps:
        swap.wait_send()

    @pl.when(me + 1 < parts)
    def _():
        tail.wait_send()

    line.sent()
    gated_line.sent()
    pltpu.make_async_copy(arrived, arrived, sum_send).wait()


def on_device(
    hidden_in, norm_gain, weight_in, filter_taps, filter_decay, skip_gain, tail_cache, output_weight
):
    shards, parts = lax.axis_size("tensor"), lax.axis_size("ctx")
    rows = hidden_in.shape[0]
    depth, _, channels = weight_in.shape
    groups, taps = filter_taps.shape
    columns = output_weight.shape[1]
    all_rows = shards * rows
    chunk = min(256, channels)
    chunks = channels // chunk
    normed = normalize_rows(hidden_in, norm_gain)
    first = first_rows(filter_taps, filter_decay)
    tail = jnp.pad(tail_cache, ((1, 0), (0, 0)))
    vmem, anywhere = pl.BlockSpec(memory_space=pltpu.VMEM), pl.BlockSpec(memory_space=pl.ANY)
    dma = pltpu.SemaphoreType.DMA
    bf16, f32 = jnp.bfloat16, jnp.float32
    return pl.pallas_call(
        functools.partial(mixer_kernel, shards, parts),
        out_shape=jax.ShapeDtypeStruct((all_rows, columns), bf16),
        in_specs=[vmem, anywhere, vmem, vmem, anywhere, anywhere],
        out_specs=vmem,
        scratch_shapes=[
            pltpu.VMEM((3, depth, channels), bf16),
            pltpu.VMEM((shards, parts * rows, depth), bf16),
            pltpu.VMEM((3, shards, parts * rows, channels), bf16),
            pltpu.VMEM((3, parts - 1, all_rows, channels), bf16),
            pltpu.VMEM((all_rows, channels), f32),
            pltpu.VMEM((all_rows, channels), bf16),
            pltpu.VMEM((taps, channels), bf16),
            pltpu.VMEM((groups, taps, 2 * taps), bf16),
            pltpu.VMEM(output_weight.shape, bf16),
            pltpu.VMEM((shards, chunks, all_rows, chunk), bf16),
            pltpu.VMEM((all_rows, columns), f32),
            dma((5,)),
            dma,
            dma((parts - 1,)),
            dma((parts - 1,)),
            dma((2, shards, parts)),
            dma((shards, parts)),
            dma,
            dma((3,)),
            dma,
            dma,
            dma((2, shards, chunks)),
            dma((shards, chunks)),
        ],
        compiler_params=pltpu.CompilerParams(
            collective_id=0, has_side_effects=True, vmem_limit_bytes=60 << 20
        ),
    )(
        normed,
        weight_in.transpose(1, 0, 2),
        first,
        skip_gain.reshape(1, channels),
        tail,
        output_weight,
    )


def solution(mesh):
    in_specs = (
        P(("prompt", "ctx", "tensor"), None),
        P(),
        P("ctx", None, "tensor"),
        P("tensor", None),
        P("tensor"),
        P("tensor"),
        P("prompt", "tensor"),
        P(None, "tensor"),
    )
    out_specs = P(("prompt", "ctx"), "tensor")
    return jax.shard_map(
        on_device, mesh=mesh, in_specs=in_specs, out_specs=out_specs, check_vma=False
    )
```
